32 devices in a mesh: cfg: 2 (over y), src: 4 (over z), col: 2 (over x), half: 2 (over core).
Axes of the slice: x: 2, y: 2, z: 4, core: 2. Of those that a mesh axis runs over, the one named last changes fastest.
Arguments:
- perambulator: bfloat16 [8, 4, 2, 512, 512], P(('cfg', 'src'), None, None, ('col', 'half')), parts along dimension 0, may hold values from -0.25 to 0.25
- elemental: bfloat16 [1, 8, 2, 128, 128], P(None, ('cfg', 'src')), parts along dimension 1, may hold values from -0.5 to 0.5
- source_order: int32 [8], P('cfg'), parts along dimension 0, may hold values from 0 to 3, as said below
- column_order: int32 [8, 128], P(('cfg', 'src')), parts along dimension 0, may hold values from 0 to 127, each once within a row
Outputs:
- meson_matrix: float32 [8, 2, 1, 1, 4], P(('cfg', 'src')), parts along dimension 0
The draws below stay inside these ranges and needn't reach their ends.
There are 2 independent parts, one for each index of `cfg`. The reference program is written for one: setup_inputs(seed, part) draws one part's arguments, and reference() takes and returns one part's arrays. A program takes and returns all parts, laid end to end along the dimension named above; each array names one. Nothing has to cross between parts.
Inputs may be any that keep to these rules, and one draw needn't show every extreme that they name: `source_order`: each of 0 to 3 appears once. `column_order`: each row holds each of 0 to 127 once.
All inputs are finite; a program needn't handle non-finite values.
Results may differ from the reference program's by a relative error of at most 0.0042.
Values may be sent and summed in bfloat16 or wider, within the bound.
A program may use at most 128 MiB of HBM per device.

```python
import jax
import jax.numpy as jnp
from jax import lax

NEV = 128
NOP = 1
DIM = 512
NT = 4


def draw_source_order(key, part):
    shuffled = jax.random.permutation(jax.random.fold_in(key, 11), NT).astype(jnp.int32)
    target = (jnp.asarray(part, jnp.int32) % NT).astype(jnp.int32)
    where_target = jnp.argmax((shuffled == target).astype(jnp.int32)).astype(jnp.int32)
    first_value = shuffled[0]
    swapped = shuffled.at[where_target].set(first_value)
    return swapped.at[0].set(target)


def shard_levels(own_key, dims, shards, least, largest):
    level, own = 1.0, jax.random.fold_in(own_key, 6)
    for dim, blocks in shards:
        steps = jnp.exp(jax.random.uniform(jax.random.fold_in(own, dim), (blocks,), jnp.float32, least / len(shards), largest / len(shards)))
        level = level * jnp.repeat(steps, dims[dim] // blocks).reshape([-1 if axis == dim else 1 for axis in range(len(dims))])
    return level


def gaussian(own_key, shape, width, bound, cuts=(), kind=jnp.bfloat16):
    entries = width * jax.random.normal(own_key, shape, jnp.float32)
    if cuts:
        entries = entries * shard_levels(own_key, shape, cuts, -0.22, 0.18)
    return jnp.clip(entries, -bound, bound).astype(kind)


def setup_inputs(seed: int = 0, part: int = 0) -> dict:
    key_list = jax.random.split(jax.random.key(seed), 5)
    own_keys = jax.random.split(jax.random.fold_in(key_list[4], part), 5)
    perambulator = gaussian(own_keys[0], (NT, NT, 2, DIM, DIM), (DIM ** -0.5), 0.25, ((0, 4), (3, 4)))
    elemental = gaussian(own_keys[1], (NOP, NT, 2, NEV, NEV), NEV ** -0.5, 0.5, ((1, 4),))
    source_order = draw_source_order(jax.random.fold_in(jax.random.fold_in(key_list[4], part), 71), part)
    column_order = jax.vmap(lambda own: jax.random.permutation(own, NEV))(jax.random.split(own_keys[3], NT)).reshape((NT, NEV)).astype(jnp.int32)
    return dict(perambulator=perambulator, elemental=elemental, source_order=source_order, column_order=column_order)


spin_sign = (1.0, 1.0, -1.0, -1.0)


def apply_rows(coefficients, tiles):
    slot_count = tiles.shape[0]
    column_count = tiles.shape[2]
    coef_real = coefficients[:, :, 0].astype(jnp.float32)
    coef_imag = coefficients[:, :, 1].astype(jnp.float32)
    tile_view = tiles.astype(jnp.float32).reshape(slot_count, 2, column_count, 4, NEV)
    tile_real = tile_view[:, 0]
    tile_imag = tile_view[:, 1]
    form = "qomr,qjsr->qosmj"
    highest = lax.Precision.HIGHEST
    real_part = jnp.einsum(form, coef_real, tile_real, precision=highest) - jnp.einsum(form, coef_imag, tile_imag, precision=highest)
    imag_part = jnp.einsum(form, coef_real, tile_imag, precision=highest) + jnp.einsum(form, coef_imag, tile_real, precision=highest)
    sign_table = jnp.array(spin_sign, jnp.float32)[:, None, None]
    stacked = jnp.stack([real_part * sign_table, imag_part * sign_table], axis=2)
    return stacked.reshape(slot_count, coefficients.shape[1], 2, 4 * NEV, column_count).astype(jnp.bfloat16)


def reference(perambulator, elemental, source_order, column_order):
    reordered = jax.vmap(lambda matrices, ordering: matrices[:, :, ordering, :], in_axes=(1, 0), out_axes=1)(elemental, column_order)
    by_slot = jnp.moveaxis(reordered, 1, 0)

    def one_source(slot):
        forward = apply_rows(by_slot, jnp.take(perambulator[slot], source_order, axis=0))
        own_coef = jnp.broadcast_to(by_slot[slot], by_slot.shape)
        backward = apply_rows(own_coef, jnp.take(perambulator, source_order[slot], axis=1))
        pair_sums = jnp.einsum("qaxij,qbyji->qabxy", forward.astype(jnp.float32), backward.astype(jnp.float32), precision=lax.Precision.HIGHEST)
        real_part = pair_sums[..., 0, 0] - pair_sums[..., 1, 1]
        imag_part = pair_sums[..., 0, 1] + pair_sums[..., 1, 0]
        return jnp.transpose(jnp.stack([real_part, imag_part], 0), (0, 2, 3, 1))

    return lax.map(one_source, jnp.arange(NT, dtype=jnp.int32))
```

```python
import functools

import jax
import jax.numpy as jnp
from jax import lax
from jax.experimental import pallas as pl
from jax.experimental.pallas import tpu as pltpu
from jax.sharding import PartitionSpec as P

spin_sign = (1.0, 1.0, -1.0, -1.0)
MESH = pl.DeviceIdType.MESH
NT = (((1,), (1,)), ((), ()))


def dot_nt(a, b):
    return lax.dot_general(a, b, NT, preferred_element_type=jnp.float32)


def sends(source, target):
    even = lax.rem(source + target, 2) == 0
    return jnp.logical_and(even, source < target) | jnp.logical_and(
        jnp.logical_not(even), source > target
    )


def kernel(
    sizes,
    tiles_hbm, elem_hbm, order_hbm, column_hbm,
    out_ref,
    tiles, elem, order, column,
    sorted_tiles, coef, mirror, result,
    load_sem, tile_send, tile_recv, coef_send, coef_recv, share_send, share_recv,
    result_send, result_recv,
):
    src_count, col_count, half_count = sizes
    blocks = col_count * half_count
    block_cols, components = tiles.shape[2], tiles.shape[3]
    eigen = elem.shape[-1]
    spins = components // eigen
    piece = eigen // blocks
    p = lax.axis_index("src")
    b = lax.axis_index("col") * half_count + lax.axis_index("half")

    def device(slot, block):
        return {
            "src": slot,
            "col": lax.div(block, half_count),
            "half": lax.rem(block, half_count),
        }

    def wait_bytes(ref, sem):
        pltpu.make_async_copy(ref, ref, sem).wait()

    barrier = pltpu.get_barrier_semaphore()
    count = src_count * blocks
    me = p * blocks + b

    @pl.loop(1, count)
    def _(step):
        other = lax.rem(me + step, count)
        pl.semaphore_signal(
            barrier,
            inc=1,
            device_id=device(lax.div(other, blocks), lax.rem(other, blocks)),
            device_id_type=MESH,
        )

    loads = [
        pltpu.make_async_copy(order_hbm, order, load_sem.at[0]),
        pltpu.make_async_copy(tiles_hbm.at[0], tiles, load_sem.at[1]),
        pltpu.make_async_copy(elem_hbm.at[0, 0], elem, load_sem.at[2]),
        pltpu.make_async_copy(column_hbm, column, load_sem.at[3]),
    ]
    for load in loads:
        load.start()

    loads[2].wait()
    loads[3].wait()
    pick = (
        lax.broadcasted_iota(jnp.int32, (eigen, eigen), 0) == column[...]
    ).astype(jnp.float32).T.astype(jnp.bfloat16)
    both = jnp.concatenate([elem[0], elem[1]], axis=1)
    rows = jnp.dot(pick, both, preferred_element_type=jnp.float32).astype(jnp.bfloat16)
    coef[p, 0] = rows[:, :eigen]
    coef[p, 1] = rows[:, eigen:]

    loads[0].wait()
    loads[1].wait()

    @pl.loop(0, src_count)
    def _(slot):
        sorted_tiles[slot] = tiles[order[slot]]

    my_spin = lax.div(b * block_cols, eigen)
    my_lanes = pl.ds(pl.multiple_of(my_spin * eigen, eigen), eigen)
    my_rows = pl.ds(pl.multiple_of(b * block_cols, block_cols), block_cols)
    mirror[p, :, my_rows, :] = sorted_tiles[p, :, :, my_lanes]

    pl.semaphore_wait(barrier, count - 1)

    def partner(step):
        distance = src_count - 1 - lax.div(step, 2)
        slot = jnp.where(lax.rem(step, 2) == 0, p + distance, p - distance)
        valid = jnp.logical_and(slot >= 0, slot < src_count)
        return jnp.clip(slot, 0, src_count - 1), valid

    my_piece = pl.ds(pl.multiple_of(b * piece, piece), piece)

    def send_tile(slot, block):
        lanes = pl.ds(pl.multiple_of(lax.div(block * block_cols, eigen) * eigen, eigen), eigen)
        pltpu.make_async_remote_copy(
            src_ref=sorted_tiles.at[slot, :, :, lanes],
            dst_ref=mirror.at[p, :, my_rows, :],
            send_sem=tile_send.at[slot],
            recv_sem=tile_recv.at[p],
            device_id=device(slot, block),
            device_id_type=MESH,
        ).start()

    steps = 2 * (src_count - 1)

    @pl.loop(0, steps)
    def _(step):
        slot, valid = partner(step)

        @pl.when(jnp.logical_and(valid, sends(p, slot)))
        def _():
            pltpu.make_async_remote_copy(
                src_ref=coef.at[p, :, my_piece, :],
                dst_ref=coef.at[p, :, my_piece, :],
                send_sem=coef_send.at[slot],
                recv_sem=coef_recv.at[p],
                device_id={"src": slot},
                device_id_type=MESH,
            ).start()

    @pl.loop(0, steps)
    def _(step):
        slot, valid = partner(step)

        @pl.when(jnp.logical_and(valid, sends(p, slot)))
        def _():
            @pl.loop(0, blocks)
            def _(k):
                send_tile(slot, lax.rem(b + k, blocks))

    @pl.loop(1, blocks)
    def _(k):
        send_tile(p, lax.rem(b + k, blocks))

    @pl.loop(0, steps)
    def _(step):
        slot, valid = partner(step)

        @pl.when(jnp.logical_and(valid, sends(slot, p)))
        def _():
            wait_bytes(coef.at[slot, :, pl.ds(0, piece), :], coef_recv.at[slot])

            @pl.loop(1, blocks)
            def _(k):
                pltpu.make_async_remote_copy(
                    src_ref=coef.at[slot, :, my_piece, :],
                    dst_ref=coef.at[slot, :, my_piece, :],
                    send_sem=share_send.at[slot],
                    recv_sem=share_recv.at[slot],
                    device_id=device(p, lax.rem(b + k, blocks)),
                    device_id_type=MESH,
                ).start()

    def fold(value):
        return jnp.sum(value.reshape(block_cols // 8, 8, eigen), axis=0)

    offset = pl.ds(pl.multiple_of(lax.rem(b * block_cols, eigen), block_cols), block_cols)
    own_sign = jnp.where(my_spin < 2, spin_sign[0], spin_sign[2]).astype(jnp.float32)

    def pair(slot):
        own_real, own_imag = coef[p, 0, offset, :], coef[p, 1, offset, :]
        left = jnp.concatenate(
            [
                jnp.concatenate([own_real, -own_imag], axis=1),
                jnp.concatenate([own_imag, own_real], axis=1),
            ],
            axis=0,
        )
        far_real, far_imag = coef[slot, 0], coef[slot, 1]
        right = jnp.concatenate(
            [
                jnp.concatenate([far_real, -far_imag], axis=1),
                jnp.concatenate([far_imag, far_real], axis=1),
            ],
            axis=0,
        )
        total_real = jnp.zeros((8, eigen), jnp.float32)
        total_imag = jnp.zeros((8, eigen), jnp.float32)
        for spin in range(spins):
            part = slice(spin * eigen, (spin + 1) * eigen)
            near = jnp.concatenate(
                [sorted_tiles[slot, 0, :, part], sorted_tiles[slot, 1, :, part]], axis=1
            )
            away = jnp.concatenate([mirror[slot, 0, part, :], mirror[slot, 1, part, :]], axis=1)
            forward = dot_nt(near, right).astype(jnp.bfloat16).astype(jnp.float32)
            backward = dot_nt(left, away).astype(jnp.bfloat16).astype(jnp.float32)
            fr, fi = forward[:, :eigen], forward[:, eigen:]
            br, bi = backward[:block_cols], backward[block_cols:]
            total_real += spin_sign[spin] * fold(fr * br - fi * bi)
            total_imag += spin_sign[spin] * fold(fr * bi + fi * br)
        result[slot, b, 0] = own_sign * total_real
        result[slot, b, 1] = own_sign * total_imag

    def send_result(slot, target, block, there):
        pltpu.make_async_remote_copy(
            src_ref=result.at[slot, b],
            dst_ref=result.at[there, b],
            send_sem=result_send.at[slot],
            recv_sem=result_recv.at[there],
            device_id=device(target, block),
            device_id_type=MESH,
        ).start()

    def share_in_slot(slot):
        @pl.loop(1, blocks)
        def _(k):
            send_result(slot, p, lax.rem(b + k, blocks), slot)

    wait_bytes(mirror.at[p, :, pl.ds(0, components - block_cols), :], tile_recv.at[p])
    pair(p)
    share_in_slot(p)

    @pl.loop(0, steps)
    def _(step):
        slot, valid = partner(step)

        @pl.when(jnp.logical_and(valid, sends(slot, p)))
        def _():
            wait_bytes(coef.at[slot, :, pl.ds(0, eigen - piece), :], share_recv.at[slot])
            wait_bytes(mirror.at[slot], tile_recv.at[slot])
            pair(slot)

            @pl.loop(0, blocks)
            def _(k):
                send_result(slot, slot, lax.rem(b + k, blocks), p)

            share_in_slot(slot)

    lane = lax.broadcasted_iota(jnp.int32, (1, src_count), 1)

    def gather(slot, rows):
        real_row, imag_row = rows
        here = jnp.logical_or(slot == p, sends(slot, p))

        @pl.when(here)
        def _():
            wait_bytes(result.at[slot, pl.ds(0, blocks - 1)], result_recv.at[slot])

        @pl.when(jnp.logical_not(here))
        def _():
            wait_bytes(result.at[slot], result_recv.at[slot])

        total = jnp.sum(result[slot], axis=0)
        real_row = jnp.where(lane == slot, jnp.sum(total[0], keepdims=True), real_row)
        imag_row = jnp.where(lane == slot, jnp.sum(total[1], keepdims=True), imag_row)
        return real_row, imag_row

    zero = jnp.zeros((1, src_count), jnp.float32)
    real_row, imag_row = lax.fori_loop(0, src_count, gather, (zero, zero))
    out_ref[0, 0, 0] = real_row
    out_ref[0, 1, 0] = imag_row

    wait_bytes(mirror.at[p, :, pl.ds(0, components - block_cols), :], tile_send.at[p])
    wait_bytes(result.at[p, pl.ds(0, blocks - 1)], result_send.at[p])

    @pl.loop(0, steps)
    def _(step):
        slot, valid = partner(step)

        @pl.when(jnp.logical_and(valid, sends(p, slot)))
        def _():
            wait_bytes(coef.at[slot, :, pl.ds(0, piece), :], coef_send.at[slot])
            wait_bytes(mirror.at[slot], tile_send.at[slot])

        @pl.when(jnp.logical_and(valid, sends(slot, p)))
        def _():
            wait_bytes(coef.at[slot, :, pl.ds(0, eigen - piece), :], share_send.at[slot])
            wait_bytes(result.at[slot], result_send.at[slot])
            wait_bytes(result.at[slot, pl.ds(0, blocks - 1)], result_send.at[slot])


def on_device(sizes, perambulator, elemental, source_order, column_order):
    operators = elemental.shape[0]
    eigen = elemental.shape[-1]
    _, slots, _, block_cols, components = perambulator.shape
    src_count, col_count, half_count = sizes
    blocks = col_count * half_count
    sem = pltpu.SemaphoreType.DMA
    return pl.pallas_call(
        functools.partial(kernel, sizes),
        out_shape=jax.ShapeDtypeStruct((1, 2, operators, operators, slots), jnp.float32),
        in_specs=[pl.BlockSpec(memory_space=pl.ANY)] * 4,
        out_specs=pl.BlockSpec(memory_space=pltpu.VMEM),
        scratch_shapes=[
            pltpu.VMEM((slots, 2, block_cols, components), jnp.bfloat16),
            pltpu.VMEM((2, eigen, eigen), jnp.bfloat16),
            pltpu.SMEM((slots,), jnp.int32),
            pltpu.VMEM((1, eigen), jnp.int32),
            pltpu.VMEM((slots, 2, block_cols, components), jnp.bfloat16),
            pltpu.VMEM((slots, 2, eigen, eigen), jnp.bfloat16),
            pltpu.VMEM((slots, 2, components, eigen), jnp.bfloat16),
            pltpu.VMEM((slots, blocks, 2, 8, eigen), jnp.float32),
            sem((4,)),
        ]
        + [sem((slots,))] * 8,
        compiler_params=pltpu.CompilerParams(collective_id=0, has_side_effects=True),
    )(perambulator, elemental, source_order, column_order)


def solution(mesh):
    sizes = (mesh.shape["src"], mesh.shape["col"], mesh.shape["half"])
    return jax.shard_map(
        functools.partial(on_device, sizes),
        mesh=mesh,
        in_specs=(
            P(("cfg", "src"), None, None, ("col", "half"), None),
            P(None, ("cfg", "src"), None, None, None),
            P("cfg"),
            P(("cfg", "src"), None),
        ),
        out_specs=P(("cfg", "src"), None, None, None, None),
        check_vma=False,
    )
```

```python
import functools

import jax
import jax.numpy as jnp
from jax import lax
from jax.experimental import pallas as pl
from jax.experimental.pallas import tpu as pltpu
from jax.sharding import PartitionSpec as P

spin_sign = (1.0, 1.0, -1.0, -1.0)
MESH = pl.DeviceIdType.MESH
NT = (((1,), (1,)), ((), ()))


def dot_nt(a, b):
    return lax.dot_general(a, b, NT, preferred_element_type=jnp.float32)


def sends(source, target):
    even = lax.rem(source + target, 2) == 0
    return jnp.logical_and(even, source < target) | jnp.logical_and(
        jnp.logical_not(even), source > target
    )


def kernel(
    sizes,
    tiles_hbm, elem_hbm, order_hbm, column_hbm,
    out_ref,
    tiles, elem, order, column,
    sorted_tiles, coef, mirror, result,
    load_sem, tile_send, tile_recv, coef_send, coef_recv, share_send, share_recv,
    result_send, result_recv,
):
    src_count, col_count, half_count = sizes
    blocks = col_count * half_count
    block_cols, components = tiles.shape[2], tiles.shape[3]
    eigen = elem.shape[-1]
    spins = components // eigen
    piece = eigen // blocks
    p = lax.axis_index("src")
    b = lax.axis_index("col") * half_count + lax.axis_index("half")

    def device(slot, block):
        return {
            "src": slot,
            "col": lax.div(block, half_count),
            "half": lax.rem(block, half_count),
        }

    def wait_bytes(ref, sem):
        pltpu.make_async_copy(ref, ref, sem).wait()

    barrier = pltpu.get_barrier_semaphore()
    count = src_count * blocks
    me = p * blocks + b

    @pl.loop(1, count)
    def _(step):
        other = lax.rem(me + step, count)
        pl.semaphore_signal(
            barrier,
            inc=1,
            device_id=device(lax.div(other, blocks), lax.rem(other, blocks)),
            device_id_type=MESH,
        )

    loads = [
        pltpu.make_async_copy(order_hbm, order, load_sem.at[0]),
        pltpu.make_async_copy(tiles_hbm.at[0], tiles, load_sem.at[1]),
        pltpu.make_async_copy(elem_hbm.at[0, 0], elem, load_sem.at[2]),
        pltpu.make_async_copy(column_hbm, column, load_sem.at[3]),
    ]
    for load in loads:
        load.start()

    loads[2].wait()
    loads[3].wait()
    pick = (
        lax.broadcasted_iota(jnp.int32, (eigen, eigen), 0) == column[...]
    ).astype(jnp.float32).T.astype(jnp.bfloat16)
    both = jnp.concatenate([elem[0], elem[1]], axis=1)
    rows = jnp.dot(pick, both, preferred_element_type=jnp.float32).astype(jnp.bfloat16)
    coef[p, 0] = rows[:, :eigen]
    coef[p, 1] = rows[:, eigen:]

    loads[0].wait()
    loads[1].wait()

    @pl.loop(0, src_count)
    def _(slot):
        sorted_tiles[slot] = tiles[order[slot]]

    my_spin = lax.div(b * block_cols, eigen)
    my_lanes = pl.ds(pl.multiple_of(my_spin * eigen, eigen), eigen)
    my_rows = pl.ds(pl.multiple_of(b * block_cols, block_cols), block_cols)
    mirror[p, :, my_rows, :] = sorted_tiles[p, :, :, my_lanes]

    pl.semaphore_wait(barrier, count - 1)

    def partner(step):
        distance = 1 + lax.div(step, 2)
        slot = jnp.where(lax.rem(step, 2) == 0, p + distance, p - distance)
        valid = jnp.logical_and(slot >= 0, slot < src_count)
        return jnp.clip(slot, 0, src_count - 1), valid

    my_piece = pl.ds(pl.multiple_of(b * piece, piece), piece)

    def send_tile(slot, block):
        lanes = pl.ds(pl.multiple_of(lax.div(block * block_cols, eigen) * eigen, eigen), eigen)
        pltpu.make_async_remote_copy(
            src_ref=sorted_tiles.at[slot, :, :, lanes],
            dst_ref=mirror.at[p, :, my_rows, :],
            send_sem=tile_send.at[slot],
            recv_sem=tile_recv.at[p],
            device_id=device(slot, block),
            device_id_type=MESH,
        ).start()

    steps = 2 * (src_count - 1)

    @pl.loop(0, steps)
    def _(step):
        slot, valid = partner(step)

        @pl.when(jnp.logical_and(valid, sends(p, slot)))
        def _():
            pltpu.make_async_remote_copy(
                src_ref=coef.at[p, :, my_piece, :],
                dst_ref=coef.at[p, :, my_piece, :],
                send_sem=coef_send.at[slot],
                recv_sem=coef_recv.at[p],
                device_id={"src": slot},
                device_id_type=MESH,
            ).start()

    @pl.loop(0, steps)
    def _(step):
        slot, valid = partner(step)

        @pl.when(jnp.logical_and(valid, sends(p, slot)))
        def _():
            @pl.loop(0, blocks)
            def _(k):
                send_tile(slot, lax.rem(b + k, blocks))

    @pl.loop(1, blocks)
    def _(k):
        send_tile(p, lax.rem(b + k, blocks))

    @pl.loop(0, steps)
    def _(step):
        slot, valid = partner(step)

        @pl.when(jnp.logical_and(valid, sends(slot, p)))
        def _():
            wait_bytes(coef.at[slot, :, pl.ds(0, piece), :], coef_recv.at[slot])

            @pl.loop(1, blocks)
            def _(k):
                pltpu.make_async_remote_copy(
                    src_ref=coef.at[slot, :, my_piece, :],
                    dst_ref=coef.at[slot, :, my_piece, :],
                    send_sem=share_send.at[slot],
                    recv_sem=share_recv.at[slot],
                    device_id=device(p, lax.rem(b + k, blocks)),
                    device_id_type=MESH,
                ).start()

    def fold(value):
        return jnp.sum(value.reshape(block_cols // 8, 8, eigen), axis=0)

    offset = pl.ds(pl.multiple_of(lax.rem(b * block_cols, eigen), block_cols), block_cols)
    own_sign = jnp.where(my_spin < 2, spin_sign[0], spin_sign[2]).astype(jnp.float32)

    def pair(slot):
        own_real, own_imag = coef[p, 0, offset, :], coef[p, 1, offset, :]
        left = jnp.concatenate(
            [
                jnp.concatenate([own_real, -own_imag], axis=1),
                jnp.concatenate([own_imag, own_real], axis=1),
            ],
            axis=0,
        )
        far_real, far_imag = coef[slot, 0], coef[slot, 1]
        right = jnp.concatenate(
            [
                jnp.concatenate([far_real, -far_imag], axis=1),
                jnp.concatenate([far_imag, far_real], axis=1),
            ],
            axis=0,
        )
        total_real = jnp.zeros((8, eigen), jnp.float32)
        total_imag = jnp.zeros((8, eigen), jnp.float32)
        for spin in range(spins):
            part = slice(spin * eigen, (spin + 1) * eigen)
            near = jnp.concatenate(
                [sorted_tiles[slot, 0, :, part], sorted_tiles[slot, 1, :, part]], axis=1
            )
            away = jnp.concatenate([mirror[slot, 0, part, :], mirror[slot, 1, part, :]], axis=1)
            forward = dot_nt(near, right).astype(jnp.bfloat16).astype(jnp.float32)
            backward = dot_nt(left, away).astype(jnp.bfloat16).astype(jnp.float32)
            fr, fi = forward[:, :eigen], forward[:, eigen:]
            br, bi = backward[:block_cols], backward[block_cols:]
            total_real += spin_sign[spin] * fold(fr * br - fi * bi)
            total_imag += spin_sign[spin] * fold(fr * bi + fi * br)
        result[slot, b, 0] = own_sign * total_real
        result[slot, b, 1] = own_sign * total_imag

    def send_result(slot, target, block, there):
        pltpu.make_async_remote_copy(
            src_ref=result.at[slot, b],
            dst_ref=result.at[there, b],
            send_sem=result_send.at[slot],
            recv_sem=result_recv.at[there],
            device_id=device(target, block),
            device_id_type=MESH,
        ).start()

    def share_in_slot(slot):
        @pl.loop(1, blocks)
        def _(k):
            send_result(slot, p, lax.rem(b + k, blocks), slot)

    wait_bytes(mirror.at[p, :, pl.ds(0, components - block_cols), :], tile_recv.at[p])
    pair(p)
    share_in_slot(p)

    @pl.loop(0, steps)
    def _(step):
        slot, valid = partner(step)

        @pl.when(jnp.logical_and(valid, sends(slot, p)))
        def _():
            wait_bytes(coef.at[slot, :, pl.ds(0, eigen - piece), :], share_recv.at[slot])
            wait_bytes(mirror.at[slot], tile_recv.at[slot])
            pair(slot)

            @pl.loop(0, blocks)
            def _(k):
                send_result(slot, slot, lax.rem(b + k, blocks), p)

            share_in_slot(slot)

    lane = lax.broadcasted_iota(jnp.int32, (1, src_count), 1)

    def gather(slot, rows):
        real_row, imag_row = rows
        here = jnp.logical_or(slot == p, sends(slot, p))

        @pl.when(here)
        def _():
            wait_bytes(result.at[slot, pl.ds(0, blocks - 1)], result_recv.at[slot])

        @pl.when(jnp.logical_not(here))
        def _():
            wait_bytes(result.at[slot], result_recv.at[slot])

        total = jnp.sum(result[slot], axis=0)
        real_row = jnp.where(lane == slot, jnp.sum(total[0], keepdims=True), real_row)
        imag_row = jnp.where(lane == slot, jnp.sum(total[1], keepdims=True), imag_row)
        return real_row, imag_row

    zero = jnp.zeros((1, src_count), jnp.float32)
    real_row, imag_row = lax.fori_loop(0, src_count, gather, (zero, zero))
    out_ref[0, 0, 0] = real_row
    out_ref[0, 1, 0] = imag_row

    wait_bytes(mirror.at[p, :, pl.ds(0, components - block_cols), :], tile_send.at[p])
    wait_bytes(result.at[p, pl.ds(0, blocks - 1)], result_send.at[p])

    @pl.loop(0, steps)
    def _(step):
        slot, valid = partner(step)

        @pl.when(jnp.logical_and(valid, sends(p, slot)))
        def _():
            wait_bytes(coef.at[slot, :, pl.ds(0, piece), :], coef_send.at[slot])
            wait_bytes(mirror.at[slot], tile_send.at[slot])

        @pl.when(jnp.logical_and(valid, sends(slot, p)))
        def _():
            wait_bytes(coef.at[slot, :, pl.ds(0, eigen - piece), :], share_send.at[slot])
            wait_bytes(result.at[slot], result_send.at[slot])
            wait_bytes(result.at[slot, pl.ds(0, blocks - 1)], result_send.at[slot])


def on_device(sizes, perambulator, elemental, source_order, column_order):
    operators = elemental.shape[0]
    eigen = elemental.shape[-1]
    _, slots, _, block_cols, components = perambulator.shape
    src_count, col_count, half_count = sizes
    blocks = col_count * half_count
    sem = pltpu.SemaphoreType.DMA
    return pl.pallas_call(
        functools.partial(kernel, sizes),
        out_shape=pltpu.VMEM((1, 2, operators, operators, slots), jnp.float32),
        in_specs=[pl.BlockSpec(memory_space=pl.ANY)] * 4,
        out_specs=pl.BlockSpec(memory_space=pltpu.VMEM),
        scratch_shapes=[
            pltpu.VMEM((slots, 2, block_cols, components), jnp.bfloat16),
            pltpu.VMEM((2, eigen, eigen), jnp.bfloat16),
            pltpu.SMEM((slots,), jnp.int32),
            pltpu.VMEM((1, eigen), jnp.int32),
            pltpu.VMEM((slots, 2, block_cols, components), jnp.bfloat16),
            pltpu.VMEM((slots, 2, eigen, eigen), jnp.bfloat16),
            pltpu.VMEM((slots, 2, components, eigen), jnp.bfloat16),
            pltpu.VMEM((slots, blocks, 2, 8, eigen), jnp.float32),
            sem((4,)),
        ]
        + [sem((slots,))] * 8,
        compiler_params=pltpu.CompilerParams(collective_id=0, has_side_effects=True),
    )(perambulator, elemental, source_order, column_order)


def solution(mesh):
    sizes = (mesh.shape["src"], mesh.shape["col"], mesh.shape["half"])
    return jax.shard_map(
        functools.partial(on_device, sizes),
        mesh=mesh,
        in_specs=(
            P(("cfg", "src"), None, None, ("col", "half"), None),
            P(None, ("cfg", "src"), None, None, None),
            P("cfg"),
            P(("cfg", "src"), None),
        ),
        out_specs=P(("cfg", "src"), None, None, None, None),
        check_vma=False,
    )
```

```python
import functools

import jax
import jax.numpy as jnp
from jax import lax
from jax.experimental import pallas as pl
from jax.experimental.pallas import tpu as pltpu
from jax.sharding import PartitionSpec as P

spin_sign = (1.0, 1.0, -1.0, -1.0)
MESH = pl.DeviceIdType.MESH
NT = (((1,), (1,)), ((), ()))


def dot_nt(a, b):
    return lax.dot_general(a, b, NT, preferred_element_type=jnp.float32)


def sends(source, target):
    even = lax.rem(source + target, 2) == 0
    return jnp.logical_and(even, source < target) | jnp.logical_and(
        jnp.logical_not(even), source > target
    )


def kernel(
    sizes,
    tiles_hbm, elem_hbm, order_hbm, column_hbm,
    out_ref,
    tiles, elem, order, column,
    sorted_tiles, coef, mirror, result,
    load_sem, tile_send, tile_recv, coef_send, coef_recv, share_send, share_recv,
    result_send, result_recv,
):
    src_count, col_count, half_count = sizes
    blocks = col_count * half_count
    block_cols, components = tiles.shape[2], tiles.shape[3]
    eigen = elem.shape[-1]
    spins = components // eigen
    piece = eigen // blocks
    p = lax.axis_index("src")
    b = lax.axis_index("col") * half_count + lax.axis_index("half")

    def device(slot, block):
        return {
            "src": slot,
            "col": lax.div(block, half_count),
            "half": lax.rem(block, half_count),
        }

    def wait_bytes(ref, sem):
        pltpu.make_async_copy(ref, ref, sem).wait()

    barrier = pltpu.get_barrier_semaphore()
    count = src_count * blocks
    me = p * blocks + b

    @pl.loop(1, count)
    def _(step):
        other = lax.rem(me + step, count)
        pl.semaphore_signal(
            barrier,
            inc=1,
            device_id=device(lax.div(other, blocks), lax.rem(other, blocks)),
            device_id_type=MESH,
        )

    loads = [
        pltpu.make_async_copy(order_hbm, order, load_sem.at[0]),
        pltpu.make_async_copy(tiles_hbm.at[0], tiles, load_sem.at[1]),
        pltpu.make_async_copy(elem_hbm.at[0, 0], elem, load_sem.at[2]),
        pltpu.make_async_copy(column_hbm, column, load_sem.at[3]),
    ]
    for load in loads:
        load.start()

    loads[2].wait()
    loads[3].wait()
    pick = (
        lax.broadcasted_iota(jnp.int32, (eigen, eigen), 0) == column[...]
    ).astype(jnp.float32).T.astype(jnp.bfloat16)
    both = jnp.concatenate([elem[0], elem[1]], axis=1)
    rows = jnp.dot(pick, both, preferred_element_type=jnp.float32).astype(jnp.bfloat16)
    coef[p, 0] = rows[:, :eigen]
    coef[p, 1] = rows[:, eigen:]

    loads[0].wait()
    loads[1].wait()

    @pl.loop(0, src_count)
    def _(slot):
        sorted_tiles[slot] = tiles[order[slot]]

    my_spin = lax.div(b * block_cols, eigen)
    my_lanes = pl.ds(pl.multiple_of(my_spin * eigen, eigen), eigen)
    my_rows = pl.ds(pl.multiple_of(b * block_cols, block_cols), block_cols)
    mirror[p, :, my_rows, :] = sorted_tiles[p, :, :, my_lanes]

    pl.semaphore_wait(barrier, count - 1)

    def partner(step):
        distance = 1 + lax.div(step, 2)
        slot = jnp.where(lax.rem(step, 2) == 0, p + distance, p - distance)
        valid = jnp.logical_and(slot >= 0, slot < src_count)
        return jnp.clip(slot, 0, src_count - 1), valid

    my_piece = pl.ds(pl.multiple_of(b * piece, piece), piece)

    def send_tile(slot, block):
        lanes = pl.ds(pl.multiple_of(lax.div(block * block_cols, eigen) * eigen, eigen), eigen)
        pltpu.make_async_remote_copy(
            src_ref=sorted_tiles.at[slot, :, :, lanes],
            dst_ref=mirror.at[p, :, my_rows, :],
            send_sem=tile_send.at[slot],
            recv_sem=tile_recv.at[p],
            device_id=device(slot, block),
            device_id_type=MESH,
        ).start()

    steps = 2 * (src_count - 1)

    @pl.loop(0, steps)
    def _(step):
        slot, valid = partner(step)

        @pl.when(jnp.logical_and(valid, sends(p, slot)))
        def _():
            pltpu.make_async_remote_copy(
                src_ref=coef.at[p, :, my_piece, :],
                dst_ref=coef.at[p, :, my_piece, :],
                send_sem=coef_send.at[slot],
                recv_sem=coef_recv.at[p],
                device_id={"src": slot},
                device_id_type=MESH,
            ).start()

    @pl.loop(0, steps)
    def _(step):
        slot, valid = partner(step)

        @pl.when(jnp.logical_and(valid, sends(p, slot)))
        def _():
            @pl.loop(0, blocks)
            def _(k):
                send_tile(slot, lax.rem(b + k, blocks))

    @pl.loop(1, blocks)
    def _(k):
        send_tile(p, lax.rem(b + k, blocks))

    @pl.loop(0, steps)
    def _(step):
        slot, valid = partner(step)

        @pl.when(jnp.logical_and(valid, sends(slot, p)))
        def _():
            wait_bytes(coef.at[slot, :, pl.ds(0, piece), :], coef_recv.at[slot])

            @pl.loop(1, blocks)
            def _(k):
                pltpu.make_async_remote_copy(
                    src_ref=coef.at[slot, :, my_piece, :],
                    dst_ref=coef.at[slot, :, my_piece, :],
                    send_sem=share_send.at[slot],
                    recv_sem=share_recv.at[slot],
                    device_id=device(p, lax.rem(b + k, blocks)),
                    device_id_type=MESH,
                ).start()

    def fold(value):
        return jnp.sum(value.reshape(block_cols // 8, 8, eigen), axis=0)

    offset = pl.ds(pl.multiple_of(lax.rem(b * block_cols, eigen), block_cols), block_cols)
    own_sign = jnp.where(my_spin < 2, spin_sign[0], spin_sign[2]).astype(jnp.float32)

    def pair(slot):
        own_real, own_imag = coef[p, 0, offset, :], coef[p, 1, offset, :]
        left = jnp.concatenate(
            [
                jnp.concatenate([own_real, -own_imag], axis=1),
                jnp.concatenate([own_imag, own_real], axis=1),
            ],
            axis=0,
        )
        far_real, far_imag = coef[slot, 0], coef[slot, 1]
        right = jnp.concatenate(
            [
                jnp.concatenate([far_real, -far_imag], axis=1),
                jnp.concatenate([far_imag, far_real], axis=1),
            ],
            axis=0,
        )
        total_real = jnp.zeros((8, eigen), jnp.float32)
        total_imag = jnp.zeros((8, eigen), jnp.float32)
        for spin in range(spins):
            part = slice(spin * eigen, (spin + 1) * eigen)
            near = jnp.concatenate(
                [sorted_tiles[slot, 0, :, part], sorted_tiles[slot, 1, :, part]], axis=1
            )
            away = jnp.concatenate([mirror[slot, 0, part, :], mirror[slot, 1, part, :]], axis=1)
            forward = dot_nt(near, right).astype(jnp.bfloat16).astype(jnp.float32)
            backward = dot_nt(left, away).astype(jnp.bfloat16).astype(jnp.float32)
            fr, fi = forward[:, :eigen], forward[:, eigen:]
            br, bi = backward[:block_cols], backward[block_cols:]
            total_real += spin_sign[spin] * fold(fr * br - fi * bi)
            total_imag += spin_sign[spin] * fold(fr * bi + fi * br)
        result[slot, b, 0] = own_sign * total_real
        result[slot, b, 1] = own_sign * total_imag

    def send_result(slot, target, block, there):
        pltpu.make_async_remote_copy(
            src_ref=result.at[slot, b],
            dst_ref=result.at[there, b],
            send_sem=result_send.at[slot],
            recv_sem=result_recv.at[there],
            device_id=device(target, block),
            device_id_type=MESH,
        ).start()

    def share_in_slot(slot):
        @pl.loop(1, blocks)
        def _(k):
            send_result(slot, p, lax.rem(b + k, blocks), slot)

    wait_bytes(mirror.at[p, :, pl.ds(0, components - block_cols), :], tile_recv.at[p])
    pair(p)
    share_in_slot(p)

    @pl.loop(0, steps)
    def _(step):
        slot, valid = partner(step)

        @pl.when(jnp.logical_and(valid, sends(slot, p)))
        def _():
            wait_bytes(coef.at[slot, :, pl.ds(0, eigen - piece), :], share_recv.at[slot])
            wait_bytes(mirror.at[slot], tile_recv.at[slot])
            pair(slot)

            @pl.loop(0, blocks)
            def _(k):
                send_result(slot, slot, lax.rem(b + k, blocks), p)

            share_in_slot(slot)

    wait_bytes(mirror.at[p, :, pl.ds(0, components - block_cols), :], tile_send.at[p])
    wait_bytes(result.at[p, pl.ds(0, blocks - 1)], result_send.at[p])

    @pl.loop(0, steps)
    def _(step):
        slot, valid = partner(step)

        @pl.when(jnp.logical_and(valid, sends(p, slot)))
        def _():
            wait_bytes(coef.at[slot, :, pl.ds(0, piece), :], coef_send.at[slot])
            wait_bytes(mirror.at[slot], tile_send.at[slot])

        @pl.when(jnp.logical_and(valid, sends(slot, p)))
        def _():
            wait_bytes(coef.at[slot, :, pl.ds(0, eigen - piece), :], share_send.at[slot])
            wait_bytes(result.at[slot], result_send.at[slot])
            wait_bytes(result.at[slot, pl.ds(0, blocks - 1)], result_send.at[slot])

    @pl.loop(0, src_count)
    def _(slot):
        here = jnp.logical_or(slot == p, sends(slot, p))

        @pl.when(here)
        def _():
            wait_bytes(result.at[slot, pl.ds(0, blocks - 1)], result_recv.at[slot])

        @pl.when(jnp.logical_not(here))
        def _():
            wait_bytes(result.at[slot], result_recv.at[slot])

    lane = lax.broadcasted_iota(jnp.int32, (1, src_count), 1)
    rows = [jnp.zeros((1, src_count), jnp.float32)] * 2
    for slot in range(src_count):
        total = jnp.sum(result[slot], axis=0)
        for part in (0, 1):
            rows[part] = jnp.where(lane == slot, jnp.sum(total[part], keepdims=True), rows[part])
    out_ref[0, 0, 0] = rows[0]
    out_ref[0, 1, 0] = rows[1]


def on_device(sizes, perambulator, elemental, source_order, column_order):
    operators = elemental.shape[0]
    eigen = elemental.shape[-1]
    _, slots, _, block_cols, components = perambulator.shape
    src_count, col_count, half_count = sizes
    blocks = col_count * half_count
    sem = pltpu.SemaphoreType.DMA
    return pl.pallas_call(
        functools.partial(kernel, sizes),
        out_shape=pltpu.VMEM((1, 2, operators, operators, slots), jnp.float32),
        in_specs=[pl.BlockSpec(memory_space=pl.ANY)] * 4,
        out_specs=pl.BlockSpec(memory_space=pltpu.VMEM),
        scratch_shapes=[
            pltpu.VMEM((slots, 2, block_cols, components), jnp.bfloat16),
            pltpu.VMEM((2, eigen, eigen), jnp.bfloat16),
            pltpu.SMEM((slots,), jnp.int32),
            pltpu.VMEM((1, eigen), jnp.int32),
            pltpu.VMEM((slots, 2, block_cols, components), jnp.bfloat16),
            pltpu.VMEM((slots, 2, eigen, eigen), jnp.bfloat16),
            pltpu.VMEM((slots, 2, components, eigen), jnp.bfloat16),
            pltpu.VMEM((slots, blocks, 2, 8, eigen), jnp.float32),
            sem((4,)),
        ]
        + [sem((slots,))] * 8,
        compiler_params=pltpu.CompilerParams(collective_id=0, has_side_effects=True),
    )(perambulator, elemental, source_order, column_order)


def solution(mesh):
    sizes = (mesh.shape["src"], mesh.shape["col"], mesh.shape["half"])
    return jax.shard_map(
        functools.partial(on_device, sizes),
        mesh=mesh,
        in_specs=(
            P(("cfg", "src"), None, None, ("col", "half"), None),
            P(None, ("cfg", "src"), None, None, None),
            P("cfg"),
            P(("cfg", "src"), None),
        ),
        out_specs=P(("cfg", "src"), None, None, None, None),
        check_vma=False,
    )
```

```python
import functools

import jax
import jax.numpy as jnp
from jax import lax
from jax.experimental import pallas as pl
from jax.experimental.pallas import tpu as pltpu
from jax.sharding import PartitionSpec as P

spin_sign = (1.0, 1.0, -1.0, -1.0)
MESH = pl.DeviceIdType.MESH
NT = (((1,), (1,)), ((), ()))


def dot_nt(a, b):
    return lax.dot_general(a, b, NT, preferred_element_type=jnp.float32)


def sends(source, target):
    even = lax.rem(source + target, 2) == 0
    return jnp.logical_and(even, source < target) | jnp.logical_and(
        jnp.logical_not(even), source > target
    )


def kernel(
    sizes,
    tiles_hbm, elem_hbm, order_hbm, column_hbm,
    out_ref,
    tiles, elem, order, column,
    sorted_tiles, coef, mirror, result,
    load_sem, tile_send, tile_recv, coef_send, coef_recv, share_send, share_recv,
    result_send, result_recv,
):
    src_count, col_count, half_count = sizes
    blocks = col_count * half_count
    block_cols, components = tiles.shape[2], tiles.shape[3]
    eigen = elem.shape[-1]
    spins = components // eigen
    piece = eigen // blocks
    p = lax.axis_index("src")
    b = lax.axis_index("col") * half_count + lax.axis_index("half")

    def device(slot, block):
        return {
            "src": slot,
            "col": lax.div(block, half_count),
            "half": lax.rem(block, half_count),
        }

    def wait_bytes(ref, sem):
        pltpu.make_async_copy(ref, ref, sem).wait()

    barrier = pltpu.get_barrier_semaphore()
    count = src_count * blocks
    me = p * blocks + b

    @pl.loop(1, count, unroll=count <= 16)
    def _(step):
        other = lax.rem(me + step, count)
        pl.semaphore_signal(
            barrier,
            inc=1,
            device_id=device(lax.div(other, blocks), lax.rem(other, blocks)),
            device_id_type=MESH,
        )

    loads = [
        pltpu.make_async_copy(order_hbm, order, load_sem.at[0]),
        pltpu.make_async_copy(tiles_hbm.at[0], tiles, load_sem.at[1]),
        pltpu.make_async_copy(elem_hbm.at[0, 0], elem, load_sem.at[2]),
        pltpu.make_async_copy(column_hbm, column, load_sem.at[3]),
    ]
    for load in loads:
        load.start()

    loads[2].wait()
    loads[3].wait()
    pick = (
        lax.broadcasted_iota(jnp.int32, (eigen, eigen), 0) == column[...]
    ).astype(jnp.float32).T.astype(jnp.bfloat16)
    both = jnp.concatenate([elem[0], elem[1]], axis=1)
    rows = jnp.dot(pick, both, preferred_element_type=jnp.float32).astype(jnp.bfloat16)
    coef[p, 0] = rows[:, :eigen]
    coef[p, 1] = rows[:, eigen:]

    loads[0].wait()
    loads[1].wait()

    @pl.loop(0, src_count)
    def _(slot):
        sorted_tiles[slot] = tiles[order[slot]]

    my_spin = lax.div(b * block_cols, eigen)
    my_lanes = pl.ds(pl.multiple_of(my_spin * eigen, eigen), eigen)
    my_rows = pl.ds(pl.multiple_of(b * block_cols, block_cols), block_cols)
    mirror[p, :, my_rows, :] = sorted_tiles[p, :, :, my_lanes]

    pl.semaphore_wait(barrier, count - 1)

    def partner(step):
        distance = 1 + lax.div(step, 2)
        slot = jnp.where(lax.rem(step, 2) == 0, p + distance, p - distance)
        valid = jnp.logical_and(slot >= 0, slot < src_count)
        return jnp.clip(slot, 0, src_count - 1), valid

    my_piece = pl.ds(pl.multiple_of(b * piece, piece), piece)

    def send_tile(slot, block):
        lanes = pl.ds(pl.multiple_of(lax.div(block * block_cols, eigen) * eigen, eigen), eigen)
        pltpu.make_async_remote_copy(
            src_ref=sorted_tiles.at[slot, :, :, lanes],
            dst_ref=mirror.at[p, :, my_rows, :],
            send_sem=tile_send.at[slot],
            recv_sem=tile_recv.at[p],
            device_id=device(slot, block),
            device_id_type=MESH,
        ).start()

    steps = 2 * (src_count - 1)

    @pl.loop(0, steps)
    def _(step):
        slot, valid = partner(step)

        @pl.when(jnp.logical_and(valid, sends(p, slot)))
        def _():
            pltpu.make_async_remote_copy(
                src_ref=coef.at[p, :, my_piece, :],
                dst_ref=coef.at[p, :, my_piece, :],
                send_sem=coef_send.at[slot],
                recv_sem=coef_recv.at[p],
                device_id={"src": slot},
                device_id_type=MESH,
            ).start()

    @pl.loop(0, steps)
    def _(step):
        slot, valid = partner(step)

        @pl.when(jnp.logical_and(valid, sends(p, slot)))
        def _():
            @pl.loop(0, blocks)
            def _(k):
                send_tile(slot, lax.rem(b + k, blocks))

    @pl.loop(1, blocks)
    def _(k):
        send_tile(p, lax.rem(b + k, blocks))

    @pl.loop(0, steps)
    def _(step):
        slot, valid = partner(step)

        @pl.when(jnp.logical_and(valid, sends(slot, p)))
        def _():
            wait_bytes(coef.at[slot, :, pl.ds(0, piece), :], coef_recv.at[slot])

            @pl.loop(1, blocks)
            def _(k):
                pltpu.make_async_remote_copy(
                    src_ref=coef.at[slot, :, my_piece, :],
                    dst_ref=coef.at[slot, :, my_piece, :],
                    send_sem=share_send.at[slot],
                    recv_sem=share_recv.at[slot],
                    device_id=device(p, lax.rem(b + k, blocks)),
                    device_id_type=MESH,
                ).start()

    def fold(value):
        return jnp.sum(value.reshape(block_cols // 8, 8, eigen), axis=0)

    offset = pl.ds(pl.multiple_of(lax.rem(b * block_cols, eigen), block_cols), block_cols)
    own_sign = jnp.where(my_spin < 2, spin_sign[0], spin_sign[2]).astype(jnp.float32)

    def pair(slot):
        own_real, own_imag = coef[p, 0, offset, :], coef[p, 1, offset, :]
        left = jnp.concatenate(
            [
                jnp.concatenate([own_real, -own_imag], axis=1),
                jnp.concatenate([own_imag, own_real], axis=1),
            ],
            axis=0,
        )
        far_real, far_imag = coef[slot, 0], coef[slot, 1]
        right = jnp.concatenate(
            [
                jnp.concatenate([far_real, -far_imag], axis=1),
                jnp.concatenate([far_imag, far_real], axis=1),
            ],
            axis=0,
        )
        total_real = jnp.zeros((8, eigen), jnp.float32)
        total_imag = jnp.zeros((8, eigen), jnp.float32)
        for spin in range(spins):
            part = slice(spin * eigen, (spin + 1) * eigen)
            near = jnp.concatenate(
                [sorted_tiles[slot, 0, :, part], sorted_tiles[slot, 1, :, part]], axis=1
            )
            away = jnp.concatenate([mirror[slot, 0, part, :], mirror[slot, 1, part, :]], axis=1)
            forward = dot_nt(near, right).astype(jnp.bfloat16).astype(jnp.float32)
            backward = dot_nt(left, away).astype(jnp.bfloat16).astype(jnp.float32)
            fr, fi = forward[:, :eigen], forward[:, eigen:]
            br, bi = backward[:block_cols], backward[block_cols:]
            total_real += spin_sign[spin] * fold(fr * br - fi * bi)
            total_imag += spin_sign[spin] * fold(fr * bi + fi * br)
        result[slot, b, 0] = own_sign * total_real
        result[slot, b, 1] = own_sign * total_imag

    def send_result(slot, target, block, there):
        pltpu.make_async_remote_copy(
            src_ref=result.at[slot, b],
            dst_ref=result.at[there, b],
            send_sem=result_send.at[slot],
            recv_sem=result_recv.at[there],
            device_id=device(target, block),
            device_id_type=MESH,
        ).start()

    def share_in_slot(slot):
        @pl.loop(1, blocks)
        def _(k):
            send_result(slot, p, lax.rem(b + k, blocks), slot)

    wait_bytes(mirror.at[p, :, pl.ds(0, components - block_cols), :], tile_recv.at[p])
    pair(p)
    share_in_slot(p)

    @pl.loop(0, steps)
    def _(step):
        slot, valid = partner(step)

        @pl.when(jnp.logical_and(valid, sends(slot, p)))
        def _():
            wait_bytes(coef.at[slot, :, pl.ds(0, eigen - piece), :], share_recv.at[slot])
            wait_bytes(mirror.at[slot], tile_recv.at[slot])
            pair(slot)

            @pl.loop(0, blocks)
            def _(k):
                send_result(slot, slot, lax.rem(b + k, blocks), p)

            share_in_slot(slot)

    wait_bytes(mirror.at[p, :, pl.ds(0, components - block_cols), :], tile_send.at[p])
    wait_bytes(result.at[p, pl.ds(0, blocks - 1)], result_send.at[p])

    @pl.loop(0, steps)
    def _(step):
        slot, valid = partner(step)

        @pl.when(jnp.logical_and(valid, sends(p, slot)))
        def _():
            wait_bytes(coef.at[slot, :, pl.ds(0, piece), :], coef_send.at[slot])
            wait_bytes(mirror.at[slot], tile_send.at[slot])

        @pl.when(jnp.logical_and(valid, sends(slot, p)))
        def _():
            wait_bytes(coef.at[slot, :, pl.ds(0, eigen - piece), :], share_send.at[slot])
            wait_bytes(result.at[slot], result_send.at[slot])
            wait_bytes(result.at[slot, pl.ds(0, blocks - 1)], result_send.at[slot])

    @pl.loop(0, src_count)
    def _(slot):
        here = jnp.logical_or(slot == p, sends(slot, p))

        @pl.when(here)
        def _():
            wait_bytes(result.at[slot, pl.ds(0, blocks - 1)], result_recv.at[slot])

        @pl.when(jnp.logical_not(here))
        def _():
            wait_bytes(result.at[slot], result_recv.at[slot])

    lane = lax.broadcasted_iota(jnp.int32, (1, src_count), 1)
    rows = [jnp.zeros((1, src_count), jnp.float32)] * 2
    for slot in range(src_count):
        total = jnp.sum(result[slot], axis=0)
        for part in (0, 1):
            rows[part] = jnp.where(lane == slot, jnp.sum(total[part], keepdims=True), rows[part])
    out_ref[0, 0, 0] = rows[0]
    out_ref[0, 1, 0] = rows[1]


def on_device(sizes, perambulator, elemental, source_order, column_order):
    operators = elemental.shape[0]
    eigen = elemental.shape[-1]
    _, slots, _, block_cols, components = perambulator.shape
    src_count, col_count, half_count = sizes
    blocks = col_count * half_count
    sem = pltpu.SemaphoreType.DMA
    return pl.pallas_call(
        functools.partial(kernel, sizes),
        out_shape=pltpu.VMEM((1, 2, operators, operators, slots), jnp.float32),
        in_specs=[pl.BlockSpec(memory_space=pl.ANY)] * 4,
        out_specs=pl.BlockSpec(memory_space=pltpu.VMEM),
        scratch_shapes=[
            pltpu.VMEM((slots, 2, block_cols, components), jnp.bfloat16),
            pltpu.VMEM((2, eigen, eigen), jnp.bfloat16),
            pltpu.SMEM((slots,), jnp.int32),
            pltpu.VMEM((1, eigen), jnp.int32),
            pltpu.VMEM((slots, 2, block_cols, components), jnp.bfloat16),
            pltpu.VMEM((slots, 2, eigen, eigen), jnp.bfloat16),
            pltpu.VMEM((slots, 2, components, eigen), jnp.bfloat16),
            pltpu.VMEM((slots, blocks, 2, 8, eigen), jnp.float32),
            sem((4,)),
        ]
        + [sem((slots,))] * 8,
        compiler_params=pltpu.CompilerParams(collective_id=0, has_side_effects=True),
    )(perambulator, elemental, source_order, column_order)


def solution(mesh):
    sizes = (mesh.shape["src"], mesh.shape["col"], mesh.shape["half"])
    return jax.shard_map(
        functools.partial(on_device, sizes),
        mesh=mesh,
        in_specs=(
            P(("cfg", "src"), None, None, ("col", "half"), None),
            P(None, ("cfg", "src"), None, None, None),
            P("cfg"),
            P(("cfg", "src"), None),
        ),
        out_specs=P(("cfg", "src"), None, None, None, None),
        check_vma=False,
    )
```
